32 devices in a mesh: seq: 8 (over y, x, core), head: 4 (over z).
Axes of the slice: x: 2, y: 2, z: 4, core: 2. Of those that a mesh axis runs over, the one named last changes fastest.
Arguments:
- tokens: bfloat16 [2048, 2048], P('seq'), may hold values from -6 to 6
- w_query: bfloat16 [2048, 2048], P(None, 'head'), may hold values from -0.125 to 0.125
- w_key: bfloat16 [2048, 2048], P(None, 'head'), may hold values from -0.125 to 0.125
- w_value: bfloat16 [2048, 2048], P(None, 'head'), may hold values from -0.125 to 0.125
- w_beta: bfloat16 [2048, 16], P(None, 'head'), may hold values from -0.125 to 0.125
- b_beta: float32 [16], P('head'), may hold values from -6 to 1
- d_out: bfloat16 [2048, 2048], P('seq', 'head'), may hold values from -6 to 6
Outputs:
- d_x: bfloat16 [2048, 2048], P('seq', 'head')
- grad_query: float32 [2048, 2048], P('seq', 'head')
- grad_key: float32 [2048, 2048], P('seq', 'head')
- grad_value: float32 [2048, 2048], P('seq', 'head')
- grad_wbeta: float32 [2048, 16], P('seq', 'head')
- grad_bbeta: float32 [16], P('head')
The draws below stay inside these ranges and needn't reach their ends.
All inputs are finite; a program needn't handle non-finite values.
Results may differ from the reference program's by a relative error of at most 0.012.
Values may be sent and summed in bfloat16 or wider, within the bound.
A program may use at most 128 MiB of HBM per device.

```python
import jax
import jax.numpy as jnp
from jax import lax

H = 16
DK = 128
D = 2048
SPAN = 64
TOKENS = 2048


def with_spikes(result, key, source, target, parts, factor):
    owner, partner = [(jnp.arange(result.shape[dim]) // (result.shape[dim] // parts)).reshape([-1 if axis == dim else 1 for axis in range(result.ndim)]) for dim in (source, target)]
    chosen = jax.random.permutation(key, parts)[partner]
    strong = (owner == chosen) | (owner == (partner + parts // 2) % parts)
    return jnp.where(strong, factor * result, result)


def levels(own_key, dims, cuts, low, top_value):
    def one(position, blocks):
        draws = jax.random.uniform(jax.random.fold_in(jax.random.fold_in(own_key, 6), position), (blocks,), jnp.float32, low / len(cuts), top_value / len(cuts))
        return jnp.repeat(jnp.exp(draws), dims[position] // blocks).reshape((-1,) + (1,) * (len(dims) - position - 1))

    gain = one(*cuts[0])
    for cut in cuts[1:]:
        gain = gain * one(*cut)
    return gain


def centred(stream_key, extent, width, bound, cuts=(), held_as=jnp.bfloat16):
    values = jax.random.normal(stream_key, extent, jnp.float32) * width
    if len(cuts) > 0:
        values = levels(stream_key, extent, cuts, -0.22, 0.18) * values
    return jnp.clip(values, min=-bound, max=bound).astype(held_as)


def bell_draw_with(stream_key, extent, deviation, limit, cuts, heavy, kind=jnp.bfloat16):
    values = deviation * jax.random.normal(stream_key, extent, jnp.float32)
    if cuts:
        values = values * levels(stream_key, extent, cuts, -0.22, 0.18)
    return jnp.clip(with_spikes(values, jax.random.fold_in(stream_key, 3), *heavy), -limit, limit).astype(kind)


def setup_inputs(seed: int = 0) -> dict:
    key_list = jax.random.split(jax.random.key(seed), 8)
    tokens = bell_draw_with(key_list[0], (TOKENS, D), 1.0, 6.0, ((0, 8),), (0, 1, 8, 2.0))
    w_query = centred(key_list[1], (D, D), D ** -0.5, 0.125, ((1, 4),))
    w_key = centred(key_list[2], (D, D), D ** -0.5, 0.125, ((1, 4),))
    w_value = centred(key_list[3], (D, D), D ** -0.5, 0.125, ((1, 4),))
    w_beta = centred(key_list[4], (D, H), D ** -0.5, 0.125, ((1, 4),))
    b_beta = jnp.clip(-6.0 + 7.0 * jax.random.uniform(key_list[5], (H,), jnp.float32) ** levels(key_list[5], (H,), ((0, 4),), -0.2, 0.2), -6.0, 1.0)
    d_out = centred(key_list[6], (TOKENS, D), 1.0, 6.0, ((0, 8), (1, 4)))
    return {"tokens": tokens, "w_query": w_query, "w_key": w_key, "w_value": w_value, "w_beta": w_beta, "b_beta": b_beta, "d_out": d_out}


highest = lax.Precision.HIGHEST
epsilon = 1e-06

def delta_block(carry_state, query_block, key_block, value_block, beta_block):
    block_len = key_block.shape[1]
    strict_lower = jnp.tril(jnp.ones((block_len, block_len), key_block.dtype), -1)
    with_diagonal = jnp.tril(jnp.ones((block_len, block_len), key_block.dtype))
    weighted = beta_block[..., None] * key_block
    gram_matrix = jnp.einsum('hcd,hed->hce', weighted, key_block, precision=highest)
    system = jnp.eye(block_len, dtype=key_block.dtype) + gram_matrix * strict_lower
    w_block = lax.linalg.triangular_solve(system, weighted, left_side=True, lower=True, unit_diagonal=True)
    u_block = lax.linalg.triangular_solve(system, beta_block[..., None] * value_block, left_side=True, lower=True, unit_diagonal=True)
    updates = u_block - jnp.einsum('hcd,hvd->hcv', w_block, carry_state, precision=highest)
    scores = jnp.einsum('hcd,hed->hce', query_block, key_block, precision=highest) * with_diagonal
    outputs = jnp.einsum('hcd,hvd->hcv', query_block, carry_state, precision=highest)
    outputs = outputs + jnp.einsum('hce,hev->hcv', scores, updates, precision=highest)
    carry_state = carry_state + jnp.einsum('hcv,hcd->hvd', updates, key_block, precision=highest)
    return (carry_state, outputs, w_block)

def arrange(tensor):
    blocks_count = tensor.shape[0] // SPAN
    shaped = tensor.reshape((blocks_count, SPAN) + tensor.shape[1:])
    return jnp.swapaxes(shaped, 1, 2)

def prepare(query_raw, key_raw, value_raw, logits):
    query_norm = query_raw * lax.rsqrt(lax.optimization_barrier(jnp.sum(query_raw * query_raw, -1, keepdims=True)) + epsilon)
    key_norm = key_raw * lax.rsqrt(lax.optimization_barrier(jnp.sum(key_raw * key_raw, -1, keepdims=True)) + epsilon)
    beta_gate = 2.0 * jax.nn.sigmoid(logits)
    return (arrange(query_norm), arrange(key_norm), arrange(value_raw), arrange(beta_gate))

def delta_layer(query_raw, key_raw, value_raw, logits, initial):
    token_count, head_count, head_width = query_raw.shape
    arranged = prepare(query_raw, key_raw, value_raw, logits)

    def advance(carry_state, pieces):
        carry_state, outputs, unused = delta_block(carry_state, pieces[0], pieces[1], pieces[2], pieces[3])
        return (carry_state, outputs)
    last_state, outputs = lax.scan(jax.checkpoint(advance), initial, arranged)
    outputs = jnp.swapaxes(outputs, 1, 2).reshape(token_count, head_count, head_width)
    return (outputs, last_state)

def reference(tokens, w_query, w_key, w_value, w_beta, b_beta, d_out):
    token_count = tokens.shape[0]
    query_raw = jnp.dot(tokens.astype(jnp.float32), w_query.astype(jnp.float32), preferred_element_type=jnp.float32).reshape(token_count, H, DK)
    key_raw = jnp.dot(tokens.astype(jnp.float32), w_key.astype(jnp.float32), preferred_element_type=jnp.float32).reshape(token_count, H, DK)
    value_raw = jnp.dot(tokens.astype(jnp.float32), w_value.astype(jnp.float32), preferred_element_type=jnp.float32).reshape(token_count, H, DK)
    logits = jnp.dot(tokens.astype(jnp.float32), w_beta.astype(jnp.float32), preferred_element_type=jnp.float32) + b_beta
    initial = jnp.zeros((H, DK, DK), jnp.float32)

    def forward(first_in, second_in, third_in, fourth_in):
        return delta_layer(first_in, second_in, third_in, fourth_in, initial)[0]
    unused, pull_back = jax.vjp(forward, query_raw, key_raw, value_raw, logits)
    cotangent = d_out.astype(jnp.float32).reshape(token_count, H, DK)
    grad_q, grad_k, grad_v, grad_z = pull_back(cotangent)
    query_b = grad_q.reshape(token_count, D).astype(jnp.bfloat16)
    key_b = grad_k.reshape(token_count, D).astype(jnp.bfloat16)
    value_b = grad_v.reshape(token_count, D).astype(jnp.bfloat16)
    logit_b = grad_z.astype(jnp.bfloat16)
    input_grad = jnp.dot(query_b.astype(jnp.float32), w_query.T.astype(jnp.float32), preferred_element_type=jnp.float32)
    input_grad = input_grad + jnp.dot(key_b.astype(jnp.float32), w_key.T.astype(jnp.float32), preferred_element_type=jnp.float32)
    input_grad = input_grad + jnp.dot(value_b.astype(jnp.float32), w_value.T.astype(jnp.float32), preferred_element_type=jnp.float32)
    input_grad = input_grad + jnp.dot(logit_b.astype(jnp.float32), w_beta.T.astype(jnp.float32), preferred_element_type=jnp.float32)
    d_x = input_grad.astype(jnp.bfloat16)
    grad_query = jnp.dot(tokens.T.astype(jnp.float32), query_b.astype(jnp.float32), preferred_element_type=jnp.float32)
    grad_key = jnp.dot(tokens.T.astype(jnp.float32), key_b.astype(jnp.float32), preferred_element_type=jnp.float32)
    grad_value = jnp.dot(tokens.T.astype(jnp.float32), value_b.astype(jnp.float32), preferred_element_type=jnp.float32)
    grad_wbeta = jnp.dot(tokens.T.astype(jnp.float32), logit_b.astype(jnp.float32), preferred_element_type=jnp.float32)
    grad_bbeta = lax.optimization_barrier(jnp.sum(grad_z, 0))
    return (d_x, grad_query, grad_key, grad_value, grad_wbeta, grad_bbeta)
```

```python
import functools

import jax
import jax.numpy as jnp
from jax import lax
from jax.experimental import pallas as pl
from jax.experimental.pallas import tpu as pltpu
from jax.sharding import PartitionSpec as P

epsilon = 1e-06
LANES = 128
highest = lax.Precision.HIGHEST


def split(a):
    high = a.astype(jnp.bfloat16)
    return high, (a - high.astype(jnp.float32)).astype(jnp.bfloat16)


def only(a):
    return a.astype(jnp.bfloat16), None


def mm(a, b, dims=(1, 0)):
    numbers = (((dims[0],), (dims[1],)), ((), ()))
    dot = functools.partial(
        lax.dot_general, dimension_numbers=numbers, preferred_element_type=jnp.float32
    )
    total = dot(a[0], b[0])
    if b[1] is not None:
        total = total + dot(a[0], b[1])
    if a[1] is not None:
        total = total + dot(a[1], b[0])
    return total


def iotas(rows, cols):
    return (
        lax.broadcasted_iota(jnp.int32, (rows, cols), 0),
        lax.broadcasted_iota(jnp.int32, (rows, cols), 1),
    )


def invert_unit_lower(systems):
    size = systems[0].shape[0]
    base = min(size, LANES)
    row, col = iotas(base, base)
    eye = jnp.where(row == col, 1.0, 0.0).astype(jnp.float32)

    def step_mask(s):
        return (row // (2 * s) == col // (2 * s)) & (row % (2 * s) >= s) & (col % (2 * s) < s)

    count = size // base
    diagonals = [
        n[i * base : (i + 1) * base, i * base : (i + 1) * base] for n in systems for i in range(count)
    ]
    inverses = [eye - jnp.where(step_mask(1), n, 0.0) for n in diagonals]
    s = 2
    while s < base:
        mask = step_mask(s)
        parts = [split(x) for x in inverses]
        inner = [mm(split(jnp.where(mask, n, 0.0)), x) for n, x in zip(diagonals, parts)]
        outer = [mm(x, split(y)) for x, y in zip(parts, inner)]
        inverses = [x - y for x, y in zip(inverses, outer)]
        s *= 2
    grouped = [inverses[i * count : (i + 1) * count] for i in range(len(systems))]
    width = base
    while width < size:
        merged = []
        for n, blocks in zip(systems, grouped):
            joined = []
            for i in range(0, len(blocks), 2):
                first, second = blocks[i], blocks[i + 1]
                low = n[(i + 1) * width : (i + 2) * width, i * width : (i + 1) * width]
                corner = mm(split(second), split(mm(split(low), split(first))))
                joined.append(
                    jnp.concatenate(
                        [
                            jnp.concatenate([first, jnp.zeros_like(first)], 1),
                            jnp.concatenate([-corner, second], 1),
                        ],
                        0,
                    )
                )
            merged.append(joined)
        grouped = merged
        width *= 2
    return [g[0] for g in grouped]


def normalise(raw):
    scale = lax.rsqrt(jnp.sum(raw * raw, -1, keepdims=True) + epsilon)
    return raw * scale, scale


def summary_kernel(heads, dim, q_ref, k_ref, v_ref, z_ref, g_ref, map_ref, mid_ref):
    count = q_ref.shape[0]
    row, col = iotas(count, count)
    strict, inclusive = row > col, row >= col
    every = range(heads)
    cols = [slice(h * dim, (h + 1) * dim) for h in every]
    beta_all = 2.0 * jax.nn.sigmoid(z_ref[...])
    beta = [beta_all[:, h : h + 1] for h in every]
    qn = [normalise(q_ref[:, c])[0] for c in cols]
    kn = [normalise(k_ref[:, c])[0] for c in cols]
    ks = [split(x) for x in kn]
    qs = [split(x) for x in qn]
    gs = [(g_ref[:, c], None) for c in cols]
    gram = [jnp.where(strict, mm(x, x, (1, 1)), 0.0) for x in ks]
    inverse = [split(t) for t in invert_unit_lower([b * n for b, n in zip(beta, gram)])]
    gram = [split(n) for n in gram]
    scores = [split(jnp.where(inclusive, mm(a, b, (1, 1)), 0.0)) for a, b in zip(qs, ks)]
    back = [mm(p, g, (0, 0)) for p, g in zip(scores, gs)]
    forth_in = [jnp.concatenate([v_ref[:, c], k], 1) for c, k in zip(cols, kn)]
    forth = [split(mm(t, split(b * x))) for t, b, x in zip(inverse, beta, forth_in)]
    plain = [x - mm(n, f) for x, n, f in zip(forth_in, gram, forth)]
    adjoint = [
        mm(t, split(jnp.concatenate([p, k], 1)), (0, 0)) for t, p, k in zip(inverse, back, kn)
    ]
    ends = [mm(f, k, (0, 0)) for f, k in zip(forth, ks)]
    tails = [
        mm(g, q, (0, 0)) - mm(split(a[:, :dim]), split(b * k), (0, 0))
        for g, q, a, b, k in zip(gs, qs, adjoint, beta, kn)
    ]
    for h in every:
        map_ref[0, h] = ends[h][dim:]
        map_ref[1, h] = ends[h][:dim]
        map_ref[2, h] = tails[h]
        mid_ref[h, :, : 2 * dim] = plain[h]
        mid_ref[h, :, 2 * dim :] = adjoint[h]


def gradient_kernel(
    heads, dim, q_ref, k_ref, z_ref, g_ref, mid_ref, state_ref, adj_ref, out_ref
):
    count = q_ref.shape[0]
    row, col = iotas(count, count)
    strict, inclusive = row > col, row >= col
    beta_all = 2.0 * jax.nn.sigmoid(z_ref[...])
    width = heads * dim
    every = range(heads)
    cols = [slice(h * dim, (h + 1) * dim) for h in every]
    beta = [beta_all[:, h : h + 1] for h in every]
    qp = [normalise(q_ref[:, c]) for c in cols]
    kp = [normalise(k_ref[:, c]) for c in cols]
    ks = [split(x[0]) for x in kp]
    qs = [split(x[0]) for x in qp]
    gs = [(g_ref[:, c], None) for c in cols]
    ss = [split(state_ref[h]) for h in every]
    ds = [split(adj_ref[h]) for h in every]
    plain = [
        mid_ref[h, :, :dim] - mm(split(mid_ref[h, :, dim : 2 * dim]), ss[h], (1, 1)) for h in every
    ]
    dx = [
        mid_ref[h, :, 2 * dim : 3 * dim] + mm(split(mid_ref[h, :, 3 * dim :]), ds[h], (1, 1))
        for h in every
    ]
    us = [split(b * x) for b, x in zip(beta, plain)]
    dv = [b * x for b, x in zip(beta, dx)]
    dvs = [split(x) for x in dv]
    inner = [split(jnp.where(inclusive, mm(g, u, (1, 1)), 0.0)) for g, u in zip(gs, us)]
    pair = [jnp.where(strict, mm(d, u, (1, 1)), 0.0) for d, u in zip(dvs, us)]
    both = [split(e + e.T) for e in pair]
    dqn = [mm(g, s) + mm(i, k) for g, s, i, k in zip(gs, ss, inner, ks)]
    dkn = [
        mm(i, q, (0, 0)) + mm(u, d) - mm(x, s) - mm(e, k)
        for i, q, u, d, x, s, e, k in zip(inner, qs, us, ds, dvs, ss, both, ks)
    ]

    def through(grad, pair):
        unit, scale = pair
        return scale * (grad - unit * jnp.sum(unit * grad, -1, keepdims=True))

    lane = lax.broadcasted_iota(jnp.int32, (count, LANES), 1)
    last = jnp.zeros((count, LANES), jnp.float32)
    for h in every:
        out_ref[:, cols[h]] = through(dqn[h], qp[h]).astype(jnp.bfloat16)
        out_ref[:, width + h * dim : width + (h + 1) * dim] = through(dkn[h], kp[h]).astype(
            jnp.bfloat16
        )
        out_ref[:, 2 * width + h * dim : 2 * width + (h + 1) * dim] = dv[h].astype(jnp.bfloat16)
        dz = jnp.sum(dx[h] * plain[h], -1, keepdims=True) * beta[h] * (1.0 - 0.5 * beta[h])
        high, low = split(dz)
        last = jnp.where(lane == h, high.astype(jnp.float32), last)
        last = jnp.where(lane == heads + h, low.astype(jnp.float32), last)
    out_ref[:, 3 * width :] = last.astype(jnp.bfloat16)


def entering(part, axis, reverse):
    count = lax.axis_size(axis)
    place = lax.axis_index(axis)
    ahead = count - 1 - place if reverse else place
    gathered = lax.all_gather(part, axis)
    state = jnp.zeros_like(part[1])

    def one(lap, state):
        source = count - 1 - lap if reverse else lap
        pair = lax.dynamic_index_in_dim(gathered, source, 0, False)
        spec = "hij,hkj->hik" if reverse else "hij,hjk->hik"
        return state - jnp.einsum(spec, state, pair[0], precision=highest) + pair[1]

    return lax.fori_loop(0, ahead, one, state)


def per_device(tokens, w_query, w_key, w_value, w_beta, b_beta, d_out):
    token_count = tokens.shape[0]
    heads = w_beta.shape[1]
    width = w_query.shape[1]
    dim = width // heads
    f32 = jnp.float32
    columns = lax.all_to_all(tokens, "seq", split_axis=1, concat_axis=0, tiled=True)
    q = jnp.dot(tokens, w_query, preferred_element_type=f32)
    k = jnp.dot(tokens, w_key, preferred_element_type=f32)
    v = jnp.dot(tokens, w_value, preferred_element_type=f32)
    z = jnp.dot(tokens, w_beta, preferred_element_type=f32) + b_beta
    params = pltpu.CompilerParams(vmem_limit_bytes=60 * 1024 * 1024)
    maps, mid = pl.pallas_call(
        functools.partial(summary_kernel, heads, dim),
        out_shape=(
            jax.ShapeDtypeStruct((3, heads, dim, dim), f32),
            jax.ShapeDtypeStruct((heads, token_count, 4 * dim), f32),
        ),
        compiler_params=params,
        name="summary",
    )(q, k, v, z, d_out)
    start = entering(maps[:2], "seq", False)
    later = entering(maps[0::2], "seq", True)
    grads = pl.pallas_call(
        functools.partial(gradient_kernel, heads, dim),
        out_shape=jax.ShapeDtypeStruct((token_count, 3 * width + LANES), jnp.bfloat16),
        compiler_params=params,
        name="gradient",
    )(q, k, z, d_out, mid, start, later)
    whole = lax.all_gather(grads, "seq", axis=0, tiled=True)
    weights = (w_query, w_key, w_value)
    partial = jnp.dot(grads[:, 3 * width : 3 * width + heads], w_beta.T, preferred_element_type=f32)
    for i, w in enumerate(weights):
        partial = partial + jnp.dot(
            grads[:, i * width : (i + 1) * width], w.T, preferred_element_type=f32
        )
    d_x = lax.psum_scatter(
        partial.astype(jnp.bfloat16), "head", scatter_dimension=1, tiled=True
    )

    def weight_grad(block):
        return lax.dot_general(
            columns, block, (((0,), (0,)), ((), ())), preferred_element_type=f32
        )

    found = [weight_grad(whole[:, i * width : (i + 1) * width]) for i in range(3)]
    tail = whole[:, 3 * width :]
    grad_wbeta = weight_grad(tail)[:, :heads]
    sums = jnp.sum(tail.astype(f32), 0)
    return (d_x, *found, grad_wbeta, sums[:heads] + sums[heads : 2 * heads])


def solution(mesh):
    in_specs = (
        P("seq", None),
        P(None, "head"),
        P(None, "head"),
        P(None, "head"),
        P(None, "head"),
        P("head"),
        P("seq", "head"),
    )
    out_specs = (
        P("seq", "head"),
        P("seq", "head"),
        P("seq", "head"),
        P("seq", "head"),
        P("seq", "head"),
        P("head"),
    )
    return jax.shard_map(
        per_device, mesh=mesh, in_specs=in_specs, out_specs=out_specs, check_vma=False
    )
```

```python
import functools

import jax
import jax.numpy as jnp
from jax import lax
from jax.experimental import pallas as pl
from jax.experimental.pallas import tpu as pltpu
from jax.sharding import PartitionSpec as P

epsilon = 1e-06
LANES = 128
MESH = pl.DeviceIdType.MESH
highest = lax.Precision.HIGHEST


def split(a):
    high = a.astype(jnp.bfloat16)
    return high, (a - high.astype(jnp.float32)).astype(jnp.bfloat16)


def only(a):
    return a.astype(jnp.bfloat16), None


def mm(a, b, dims=(1, 0)):
    numbers = (((dims[0],), (dims[1],)), ((), ()))
    dot = functools.partial(
        lax.dot_general, dimension_numbers=numbers, preferred_element_type=jnp.float32
    )
    total = dot(a[0], b[0])
    if b[1] is not None:
        total = total + dot(a[0], b[1])
    if a[1] is not None:
        total = total + dot(a[1], b[0])
    return total


def iotas(rows, cols):
    return (
        lax.broadcasted_iota(jnp.int32, (rows, cols), 0),
        lax.broadcasted_iota(jnp.int32, (rows, cols), 1),
    )


def invert_unit_lower(systems):
    size = systems[0].shape[0]
    base = min(size, LANES)
    row, col = iotas(base, base)
    eye = jnp.where(row == col, 1.0, 0.0).astype(jnp.float32)

    def step_mask(s):
        return (row // (2 * s) == col // (2 * s)) & (row % (2 * s) >= s) & (col % (2 * s) < s)

    count = size // base
    diagonals = [
        n[i * base : (i + 1) * base, i * base : (i + 1) * base] for n in systems for i in range(count)
    ]
    inverses = [eye - jnp.where(step_mask(1), n, 0.0) for n in diagonals]
    s = 2
    while s < base:
        mask = step_mask(s)
        parts = [split(x) for x in inverses]
        inner = [mm(split(jnp.where(mask, n, 0.0)), x) for n, x in zip(diagonals, parts)]
        outer = [mm(x, split(y)) for x, y in zip(parts, inner)]
        inverses = [x - y for x, y in zip(inverses, outer)]
        s *= 2
    grouped = [inverses[i * count : (i + 1) * count] for i in range(len(systems))]
    width = base
    while width < size:
        merged = []
        for n, blocks in zip(systems, grouped):
            joined = []
            for i in range(0, len(blocks), 2):
                first, second = blocks[i], blocks[i + 1]
                low = n[(i + 1) * width : (i + 2) * width, i * width : (i + 1) * width]
                corner = mm(split(second), split(mm(split(low), split(first))))
                joined.append(
                    jnp.concatenate(
                        [
                            jnp.concatenate([first, jnp.zeros_like(first)], 1),
                            jnp.concatenate([-corner, second], 1),
                        ],
                        0,
                    )
                )
            merged.append(joined)
        grouped = merged
        width *= 2
    return [g[0] for g in grouped]


def normalise(raw):
    scale = lax.rsqrt(jnp.sum(raw * raw, -1, keepdims=True) + epsilon)
    return raw * scale, scale


def summary_kernel(heads, dim, q_ref, k_ref, v_ref, z_ref, g_ref, map_ref, mid_ref):
    count = q_ref.shape[0]
    row, col = iotas(count, count)
    strict, inclusive = row > col, row >= col
    every = range(heads)
    cols = [slice(h * dim, (h + 1) * dim) for h in every]
    beta_all = 2.0 * jax.nn.sigmoid(z_ref[...])
    beta = [beta_all[:, h : h + 1] for h in every]
    qn = [normalise(q_ref[:, c])[0] for c in cols]
    kn = [normalise(k_ref[:, c])[0] for c in cols]
    ks = [split(x) for x in kn]
    qs = [split(x) for x in qn]
    gs = [(g_ref[:, c], None) for c in cols]
    gram = [jnp.where(strict, mm(x, x, (1, 1)), 0.0) for x in ks]
    inverse = [split(t) for t in invert_unit_lower([b * n for b, n in zip(beta, gram)])]
    gram = [split(n) for n in gram]
    scores = [split(jnp.where(inclusive, mm(a, b, (1, 1)), 0.0)) for a, b in zip(qs, ks)]
    back = [mm(p, g, (0, 0)) for p, g in zip(scores, gs)]
    forth_in = [jnp.concatenate([v_ref[:, c], k], 1) for c, k in zip(cols, kn)]
    forth = [split(mm(t, split(b * x))) for t, b, x in zip(inverse, beta, forth_in)]
    plain = [x - mm(n, f) for x, n, f in zip(forth_in, gram, forth)]
    adjoint = [
        mm(t, split(jnp.concatenate([p, k], 1)), (0, 0)) for t, p, k in zip(inverse, back, kn)
    ]
    ends = [mm(f, k, (0, 0)) for f, k in zip(forth, ks)]
    tails = [mm(split(a), split(b * k), (0, 0)) for a, b, k in zip(adjoint, beta, kn)]
    direct = [mm(g, q, (0, 0)) for g, q in zip(gs, qs)]
    for h in every:
        map_ref[h, 0] = ends[h][dim:].astype(map_ref.dtype)
        map_ref[h, 1] = ends[h][:dim].astype(map_ref.dtype)
        map_ref[heads + h, 0] = tails[h][dim:].astype(map_ref.dtype)
        map_ref[heads + h, 1] = (direct[h] - tails[h][:dim]).astype(map_ref.dtype)
        mid_ref[h, :, : 2 * dim] = plain[h]
        mid_ref[h, :, 2 * dim :] = adjoint[h]


def gradient_kernel(
    heads, dim, q_ref, k_ref, z_ref, g_ref, mid_ref, state_ref, out_ref
):
    count = q_ref.shape[0]
    row, col = iotas(count, count)
    strict, inclusive = row > col, row >= col
    beta_all = 2.0 * jax.nn.sigmoid(z_ref[...])
    width = heads * dim
    every = range(heads)
    cols = [slice(h * dim, (h + 1) * dim) for h in every]
    beta = [beta_all[:, h : h + 1] for h in every]
    qp = [normalise(q_ref[:, c]) for c in cols]
    kp = [normalise(k_ref[:, c]) for c in cols]
    ks = [split(x[0]) for x in kp]
    qs = [split(x[0]) for x in qp]
    gs = [(g_ref[:, c], None) for c in cols]
    ss = [(state_ref[h], None) for h in every]
    ds = [(state_ref[heads + h], None) for h in every]
    plain = [
        mid_ref[h, :, :dim] - mm(split(mid_ref[h, :, dim : 2 * dim]), ss[h], (1, 1)) for h in every
    ]
    dx = [
        mid_ref[h, :, 2 * dim : 3 * dim] + mm(split(mid_ref[h, :, 3 * dim :]), ds[h], (1, 1))
        for h in every
    ]
    us = [split(b * x) for b, x in zip(beta, plain)]
    dv = [b * x for b, x in zip(beta, dx)]
    dvs = [split(x) for x in dv]
    inner = [split(jnp.where(inclusive, mm(g, u, (1, 1)), 0.0)) for g, u in zip(gs, us)]
    pair = [jnp.where(strict, mm(d, u, (1, 1)), 0.0) for d, u in zip(dvs, us)]
    both = [split(e + e.T) for e in pair]
    dqn = [mm(g, s) + mm(i, k) for g, s, i, k in zip(gs, ss, inner, ks)]
    dkn = [
        mm(i, q, (0, 0)) + mm(u, d) - mm(x, s) - mm(e, k)
        for i, q, u, d, x, s, e, k in zip(inner, qs, us, ds, dvs, ss, both, ks)
    ]

    def through(grad, pair):
        unit, scale = pair
        return scale * (grad - unit * jnp.sum(unit * grad, -1, keepdims=True))

    lane = lax.broadcasted_iota(jnp.int32, (count, LANES), 1)
    last = jnp.zeros((count, LANES), jnp.float32)
    for h in every:
        out_ref[:, cols[h]] = through(dqn[h], qp[h]).astype(jnp.bfloat16)
        out_ref[:, width + h * dim : width + (h + 1) * dim] = through(dkn[h], kp[h]).astype(
            jnp.bfloat16
        )
        out_ref[:, 2 * width + h * dim : 2 * width + (h + 1) * dim] = dv[h].astype(jnp.bfloat16)
        dz = jnp.sum(dx[h] * plain[h], -1, keepdims=True) * beta[h] * (1.0 - 0.5 * beta[h])
        high, low = split(dz)
        last = jnp.where(lane == h, high.astype(jnp.float32), last)
        last = jnp.where(lane == heads + h, low.astype(jnp.float32), last)
    out_ref[:, 3 * width :] = last.astype(jnp.bfloat16)


def gathered_states(maps, heads):
    count = lax.axis_size("seq")
    place = lax.axis_index("seq")
    gathered = lax.all_gather(maps, "seq").astype(jnp.float32)

    def walk(steps, pick, rows):
        def one(lap, state):
            pair = lax.dynamic_index_in_dim(gathered, pick(lap), 0, False)[rows]
            moved = jnp.einsum("hij,hjk->hik", state, pair[:, 0], precision=highest)
            return state - moved + pair[:, 1]

        return lax.fori_loop(0, steps, one, jnp.zeros((heads,) + maps.shape[2:], jnp.float32))

    first = walk(place, lambda lap: lap, slice(0, heads))
    second = walk(count - 1 - place, lambda lap: count - 1 - lap, slice(heads, None))
    return jnp.concatenate([first, second]).astype(maps.dtype)


def states_kernel(count, heads, map_ref, out_ref, inbox, outbox, send, recv, send_back, recv_back):
    me = lax.axis_index("seq")
    barrier = pltpu.get_barrier_semaphore()
    for r in range(1, count):
        pl.semaphore_signal(
            barrier, inc=1, device_id={"seq": lax.rem(me + r, count)}, device_id_type=MESH
        )
    pl.semaphore_wait(barrier, count - 1)
    copies = []
    for r in range(1, count):
        peer = lax.rem(me + r, count)
        copy = pltpu.make_async_remote_copy(
            src_ref=map_ref.at[peer],
            dst_ref=inbox.at[r],
            send_sem=send.at[r],
            recv_sem=recv.at[r],
            device_id={"seq": peer},
            device_id_type=MESH,
        )
        copy.start()
        copies.append(copy)
    inbox[0] = map_ref[me]
    for copy in copies:
        copy.wait()
    backward = me // heads
    state = jnp.zeros(inbox.shape[2:], jnp.float32)

    def back(p):
        source = p + backward * (count - 1 - 2 * p)
        return source, pltpu.make_async_remote_copy(
            src_ref=outbox.at[p],
            dst_ref=out_ref.at[me],
            send_sem=send_back.at[p],
            recv_sem=recv_back.at[me],
            device_id={"seq": source},
            device_id_type=MESH,
        )

    for p in range(count):
        source, copy = back(p)
        outbox[p] = state.astype(outbox.dtype)

        @pl.when(source != me)
        def _():
            copy.start()

        @pl.when(source == me)
        def _():
            out_ref[me] = outbox[p]

        if p + 1 < count:
            slot = lax.rem(me - source + count, count)
            state = state - mm(split(state), (inbox[slot, 0], None)) + inbox[slot, 1].astype(
                jnp.float32
            )
    for p in range(count):
        source, copy = back(p)

        @pl.when(source != me)
        def _():
            copy.wait_send()

    for r in range(1, count):
        unit = lax.rem(me + r, count)
        pltpu.make_async_remote_copy(
            src_ref=outbox.at[r],
            dst_ref=out_ref.at[unit],
            send_sem=send_back.at[r],
            recv_sem=recv_back.at[unit],
            device_id={"seq": unit},
            device_id_type=MESH,
        ).wait_recv()


def boundary_states(maps, heads):
    count = lax.axis_size("seq")
    units, _, dim, _ = maps.shape
    if units != count:
        return gathered_states(maps, heads)
    vmem = pl.BlockSpec(memory_space=pltpu.VMEM)
    return pl.pallas_call(
        functools.partial(states_kernel, count, heads),
        out_shape=jax.ShapeDtypeStruct((units, dim, dim), maps.dtype),
        in_specs=[vmem],
        out_specs=vmem,
        scratch_shapes=[
            pltpu.VMEM(maps.shape, maps.dtype),
            pltpu.VMEM((count, dim, dim), maps.dtype),
            pltpu.SemaphoreType.DMA((count,)),
            pltpu.SemaphoreType.DMA((count,)),
            pltpu.SemaphoreType.DMA((count,)),
            pltpu.SemaphoreType.DMA((count,)),
        ],
        compiler_params=pltpu.CompilerParams(collective_id=0, has_side_effects=True),
        name="states",
    )(maps)


def per_device(tokens, w_query, w_key, w_value, w_beta, b_beta, d_out):
    token_count = tokens.shape[0]
    heads = w_beta.shape[1]
    width = w_query.shape[1]
    dim = width // heads
    f32 = jnp.float32
    columns = lax.all_to_all(tokens, "seq", split_axis=1, concat_axis=0, tiled=True)
    q = jnp.dot(tokens, w_query, preferred_element_type=f32)
    k = jnp.dot(tokens, w_key, preferred_element_type=f32)
    v = jnp.dot(tokens, w_value, preferred_element_type=f32)
    z = jnp.dot(tokens, w_beta, preferred_element_type=f32) + b_beta
    params = pltpu.CompilerParams(vmem_limit_bytes=60 * 1024 * 1024)
    maps, mid = pl.pallas_call(
        functools.partial(summary_kernel, heads, dim),
        out_shape=(
            jax.ShapeDtypeStruct((2 * heads, 2, dim, dim), jnp.bfloat16),
            jax.ShapeDtypeStruct((heads, token_count, 4 * dim), f32),
        ),
        compiler_params=params,
        name="summary",
    )(q, k, v, z, d_out)
    states = boundary_states(maps, heads)
    grads = pl.pallas_call(
        functools.partial(gradient_kernel, heads, dim),
        out_shape=jax.ShapeDtypeStruct((token_count, 3 * width + LANES), jnp.bfloat16),
        compiler_params=params,
        name="gradient",
    )(q, k, z, d_out, mid, states)
    whole = lax.all_gather(grads, "seq", axis=0, tiled=True)
    weights = (w_query, w_key, w_value)
    partial = jnp.dot(grads[:, 3 * width : 3 * width + heads], w_beta.T, preferred_element_type=f32)
    for i, w in enumerate(weights):
        partial = partial + jnp.dot(
            grads[:, i * width : (i + 1) * width], w.T, preferred_element_type=f32
        )
    d_x = lax.psum_scatter(
        partial.astype(jnp.bfloat16), "head", scatter_dimension=1, tiled=True
    )

    def weight_grad(block):
        return lax.dot_general(
            columns, block, (((0,), (0,)), ((), ())), preferred_element_type=f32
        )

    found = [weight_grad(whole[:, i * width : (i + 1) * width]) for i in range(3)]
    tail = whole[:, 3 * width :]
    grad_wbeta = weight_grad(tail)[:, :heads]
    sums = jnp.sum(tail.astype(f32), 0)
    return (d_x, *found, grad_wbeta, sums[:heads] + sums[heads : 2 * heads])


def solution(mesh):
    in_specs = (
        P("seq", None),
        P(None, "head"),
        P(None, "head"),
        P(None, "head"),
        P(None, "head"),
        P("head"),
        P("seq", "head"),
    )
    out_specs = (
        P("seq", "head"),
        P("seq", "head"),
        P("seq", "head"),
        P("seq", "head"),
        P("seq", "head"),
        P("head"),
    )
    return jax.shard_map(
        per_device, mesh=mesh, in_specs=in_specs, out_specs=out_specs, check_vma=False
    )
```

```python
import functools

import jax
import jax.numpy as jnp
from jax import lax
from jax.experimental import pallas as pl
from jax.experimental.pallas import tpu as pltpu
from jax.sharding import PartitionSpec as P

epsilon = 1e-06
LANES = 128
MESH = pl.DeviceIdType.MESH
highest = lax.Precision.HIGHEST


def split(a):
    high = a.astype(jnp.bfloat16)
    return high, (a - high.astype(jnp.float32)).astype(jnp.bfloat16)


def only(a):
    return a.astype(jnp.bfloat16), None


def mm(a, b, dims=(1, 0)):
    numbers = (((dims[0],), (dims[1],)), ((), ()))
    dot = functools.partial(
        lax.dot_general, dimension_numbers=numbers, preferred_element_type=jnp.float32
    )
    total = dot(a[0], b[0])
    if b[1] is not None:
        total = total + dot(a[0], b[1])
    if a[1] is not None:
        total = total + dot(a[1], b[0])
    return total


def iotas(rows, cols):
    return (
        lax.broadcasted_iota(jnp.int32, (rows, cols), 0),
        lax.broadcasted_iota(jnp.int32, (rows, cols), 1),
    )


def invert_unit_lower(systems):
    size = systems[0].shape[0]
    base = min(size, LANES)
    row, col = iotas(base, base)
    eye = jnp.where(row == col, 1.0, 0.0).astype(jnp.float32)

    def step_mask(s):
        return (row // (2 * s) == col // (2 * s)) & (row % (2 * s) >= s) & (col % (2 * s) < s)

    count = size // base
    diagonals = [
        n[i * base : (i + 1) * base, i * base : (i + 1) * base] for n in systems for i in range(count)
    ]
    inverses = [eye - jnp.where(step_mask(1), n, 0.0) for n in diagonals]
    s = 2
    while s < base:
        mask = step_mask(s)
        parts = [split(x) for x in inverses]
        inner = [mm(split(jnp.where(mask, n, 0.0)), x) for n, x in zip(diagonals, parts)]
        outer = [mm(x, split(y)) for x, y in zip(parts, inner)]
        inverses = [x - y for x, y in zip(inverses, outer)]
        s *= 2
    grouped = [inverses[i * count : (i + 1) * count] for i in range(len(systems))]
    width = base
    while width < size:
        merged = []
        for n, blocks in zip(systems, grouped):
            joined = []
            for i in range(0, len(blocks), 2):
                first, second = blocks[i], blocks[i + 1]
                low = n[(i + 1) * width : (i + 2) * width, i * width : (i + 1) * width]
                corner = mm(split(second), split(mm(split(low), split(first))))
                joined.append(
                    jnp.concatenate(
                        [
                            jnp.concatenate([first, jnp.zeros_like(first)], 1),
                            jnp.concatenate([-corner, second], 1),
                        ],
                        0,
                    )
                )
            merged.append(joined)
        grouped = merged
        width *= 2
    return [g[0] for g in grouped]


def normalise(raw):
    scale = lax.rsqrt(jnp.sum(raw * raw, -1, keepdims=True) + epsilon)
    return raw * scale, scale


def meet(peers):
    barrier = pltpu.get_barrier_semaphore()
    for peer in peers:
        pl.semaphore_signal(barrier, inc=1, device_id=peer, device_id_type=MESH)
    pl.semaphore_wait(barrier, len(peers))


def exchange_summary_kernel(
    shards, heads, dim, x_ref, q_ref, k_ref, v_ref, z_ref, g_ref, map_ref, mid_ref, cols_ref, send, recv, here
):
    me = lax.axis_index("seq")
    rows = x_ref.shape[0]
    part = cols_ref.shape[1]
    peers = [lax.rem(me + r, shards) for r in range(1, shards)]
    meet([{"seq": p} for p in peers])

    def ends(p):
        return (
            x_ref.at[:, pl.ds(pl.multiple_of(p * part, part), part)],
            cols_ref.at[pl.ds(pl.multiple_of(me * rows, rows), rows), :],
        )

    copies = []
    for i, p in enumerate(peers):
        source, target = ends(p)
        copy = pltpu.make_async_remote_copy(
            src_ref=source,
            dst_ref=target,
            send_sem=send.at[i],
            recv_sem=recv.at[i],
            device_id={"seq": p},
            device_id_type=MESH,
        )
        copy.start()
        copies.append(copy)
    own = pltpu.make_async_copy(*ends(me), here)
    own.start()
    summary_kernel(heads, dim, q_ref, k_ref, v_ref, z_ref, g_ref, map_ref, mid_ref)
    own.wait()
    for copy in copies:
        copy.wait()


def finish_kernel(
    groups, grads_ref, cols_ref, wq_ref, wk_ref, wv_ref, wb_ref,
    dx_ref, gq_ref, gk_ref, gv_ref, tail_ref, sum_ref,
    held, piece, landed, send, recv, piece_send, piece_recv,
):
    me = lax.axis_index("seq")
    group = lax.axis_index("head")
    rows = grads_ref.shape[0]
    half = rows // 2
    width = gq_ref.shape[1]
    top, bottom = pl.ds(0, half), pl.ds(half, half)

    def other(o):
        index = me
        for bit in (1, 2, 4):
            if o & bit:
                index = index + bit - 2 * bit * ((me // bit) % 2)
        return index

    across, inner, outer = ({"seq": other(o)} for o in (1, 2, 4))
    others = [{"head": lax.rem(group + r, groups)} for r in range(1, groups)]
    meet([across, inner, outer] + others)

    def move(i, source, slot, part, device):
        return pltpu.make_async_remote_copy(
            src_ref=source.at[part, :],
            dst_ref=held.at[slot].at[part, :],
            send_sem=send.at[i],
            recv_sem=recv.at[i],
            device_id=device,
            device_id_type=MESH,
        )

    hops = [
        move(0, grads_ref, 1, pl.ds(0, rows), across),
        move(1, grads_ref, 2, top, inner),
        move(2, grads_ref, 2, bottom, inner),
        move(3, grads_ref, 4, bottom, outer),
        move(4, grads_ref, 4, top, outer),
        move(5, held.at[2], 6, top, outer),
        move(6, held.at[4], 6, bottom, inner),
        move(7, held.at[2], 3, top, across),
        move(8, held.at[2], 3, bottom, across),
        move(9, held.at[4], 5, top, across),
        move(10, held.at[4], 5, bottom, across),
        move(11, held.at[6], 7, top, across),
        move(12, held.at[6], 7, bottom, across),
    ]
    for i in (1, 3, 2, 4, 0):
        hops[i].start()

    def input_part(index):
        span = pl.ds(pl.multiple_of(index * width, width), width)
        total = lax.dot_general(
            grads_ref[:, 3 * width :], wb_ref[span, :], (((1,), (1,)), ((), ())),
            preferred_element_type=jnp.float32,
        )
        for i, w in enumerate((wq_ref, wk_ref, wv_ref)):
            total = total + lax.dot_general(
                grads_ref[:, i * width : (i + 1) * width], w[span, :], (((1,), (1,)), ((), ())),
                preferred_element_type=jnp.float32,
            )
        return total

    pieces = []
    for r in range(1, groups):
        piece[r] = input_part(lax.rem(group + r, groups)).astype(piece.dtype)
        copy = pltpu.make_async_remote_copy(
            src_ref=piece.at[r],
            dst_ref=landed.at[r],
            send_sem=piece_send.at[r],
            recv_sem=piece_recv.at[r],
            device_id=others[r - 1],
            device_id_type=MESH,
        )
        copy.start()
        pieces.append(copy)
    own = input_part(group)

    def add(o):
        block = grads_ref if o == 0 else held.at[o]
        span = pl.ds(pl.multiple_of(other(o) * rows, rows), rows)
        lhs = cols_ref[span, :].T
        for i, target in enumerate((gq_ref, gk_ref, gv_ref, tail_ref)):
            columns = slice(i * width, (i + 1) * width if i < 3 else None)
            value = jnp.dot(lhs, block[:, columns], preferred_element_type=jnp.float32)
            target[...] = value if o == 0 else target[...] + value
        total = jnp.sum(block[:, 3 * width :].astype(jnp.float32), 0, keepdims=True)
        sum_ref[...] = total if o == 0 else sum_ref[...] + total

    def arrive(i, *then):
        hops[i].wait_recv()
        for j in then:
            hops[j].start()

    add(0)
    arrive(0)
    add(1)
    arrive(1, 5, 7)
    arrive(3, 6, 10)
    arrive(2, 8)
    arrive(4, 9)
    add(2)
    add(4)
    arrive(7)
    arrive(8)
    add(3)
    arrive(9)
    arrive(10)
    add(5)
    for r, copy in enumerate(pieces, 1):
        copy.wait()
        own = own + landed[r].astype(jnp.float32)
    dx_ref[...] = own.astype(dx_ref.dtype)
    arrive(5, 11)
    arrive(6, 12)
    add(6)
    arrive(11)
    arrive(12)
    add(7)
    for hop in hops:
        hop.wait_send()


def summary_kernel(heads, dim, q_ref, k_ref, v_ref, z_ref, g_ref, map_ref, mid_ref):
    count = q_ref.shape[0]
    row, col = iotas(count, count)
    strict, inclusive = row > col, row >= col
    every = range(heads)
    cols = [slice(h * dim, (h + 1) * dim) for h in every]
    beta_all = 2.0 * jax.nn.sigmoid(z_ref[...])
    beta = [beta_all[:, h : h + 1] for h in every]
    qn = [normalise(q_ref[:, c])[0] for c in cols]
    kn = [normalise(k_ref[:, c])[0] for c in cols]
    ks = [split(x) for x in kn]
    qs = [split(x) for x in qn]
    gs = [(g_ref[:, c], None) for c in cols]
    gram = [jnp.where(strict, mm(x, x, (1, 1)), 0.0) for x in ks]
    inverse = [split(t) for t in invert_unit_lower([b * n for b, n in zip(beta, gram)])]
    gram = [split(n) for n in gram]
    scores = [split(jnp.where(inclusive, mm(a, b, (1, 1)), 0.0)) for a, b in zip(qs, ks)]
    back = [mm(p, g, (0, 0)) for p, g in zip(scores, gs)]
    forth_in = [jnp.concatenate([v_ref[:, c], k], 1) for c, k in zip(cols, kn)]
    forth = [split(mm(t, split(b * x))) for t, b, x in zip(inverse, beta, forth_in)]
    plain = [x - mm(n, f) for x, n, f in zip(forth_in, gram, forth)]
    adjoint = [
        mm(t, split(jnp.concatenate([p, k], 1)), (0, 0)) for t, p, k in zip(inverse, back, kn)
    ]
    ends = [mm(f, k, (0, 0)) for f, k in zip(forth, ks)]
    tails = [mm(split(a), split(b * k), (0, 0)) for a, b, k in zip(adjoint, beta, kn)]
    direct = [mm(g, q, (0, 0)) for g, q in zip(gs, qs)]
    for h in every:
        map_ref[h, 0] = ends[h][dim:].astype(map_ref.dtype)
        map_ref[h, 1] = ends[h][:dim].astype(map_ref.dtype)
        map_ref[heads + h, 0] = tails[h][dim:].astype(map_ref.dtype)
        map_ref[heads + h, 1] = (direct[h] - tails[h][:dim]).astype(map_ref.dtype)
        mid_ref[h, :, : 2 * dim] = plain[h]
        mid_ref[h, :, 2 * dim :] = adjoint[h]


def gradient_kernel(
    heads, dim, q_ref, k_ref, z_ref, g_ref, mid_ref, state_ref, out_ref
):
    count = q_ref.shape[0]
    row, col = iotas(count, count)
    strict, inclusive = row > col, row >= col
    beta_all = 2.0 * jax.nn.sigmoid(z_ref[...])
    width = heads * dim
    every = range(heads)
    cols = [slice(h * dim, (h + 1) * dim) for h in every]
    beta = [beta_all[:, h : h + 1] for h in every]
    qp = [normalise(q_ref[:, c]) for c in cols]
    kp = [normalise(k_ref[:, c]) for c in cols]
    ks = [split(x[0]) for x in kp]
    qs = [split(x[0]) for x in qp]
    gs = [(g_ref[:, c], None) for c in cols]
    ss = [(state_ref[h], None) for h in every]
    ds = [(state_ref[heads + h], None) for h in every]
    plain = [
        mid_ref[h, :, :dim] - mm(split(mid_ref[h, :, dim : 2 * dim]), ss[h], (1, 1)) for h in every
    ]
    dx = [
        mid_ref[h, :, 2 * dim : 3 * dim] + mm(split(mid_ref[h, :, 3 * dim :]), ds[h], (1, 1))
        for h in every
    ]
    us = [split(b * x) for b, x in zip(beta, plain)]
    dv = [b * x for b, x in zip(beta, dx)]
    dvs = [split(x) for x in dv]
    inner = [split(jnp.where(inclusive, mm(g, u, (1, 1)), 0.0)) for g, u in zip(gs, us)]
    pair = [jnp.where(strict, mm(d, u, (1, 1)), 0.0) for d, u in zip(dvs, us)]
    both = [split(e + e.T) for e in pair]
    dqn = [mm(g, s) + mm(i, k) for g, s, i, k in zip(gs, ss, inner, ks)]
    dkn = [
        mm(i, q, (0, 0)) + mm(u, d) - mm(x, s) - mm(e, k)
        for i, q, u, d, x, s, e, k in zip(inner, qs, us, ds, dvs, ss, both, ks)
    ]

    def through(grad, pair):
        unit, scale = pair
        return scale * (grad - unit * jnp.sum(unit * grad, -1, keepdims=True))

    lane = lax.broadcasted_iota(jnp.int32, (count, LANES), 1)
    last = jnp.zeros((count, LANES), jnp.float32)
    for h in every:
        out_ref[:, cols[h]] = through(dqn[h], qp[h]).astype(jnp.bfloat16)
        out_ref[:, width + h * dim : width + (h + 1) * dim] = through(dkn[h], kp[h]).astype(
            jnp.bfloat16
        )
        out_ref[:, 2 * width + h * dim : 2 * width + (h + 1) * dim] = dv[h].astype(jnp.bfloat16)
        dz = jnp.sum(dx[h] * plain[h], -1, keepdims=True) * beta[h] * (1.0 - 0.5 * beta[h])
        high, low = split(dz)
        last = jnp.where(lane == h, high.astype(jnp.float32), last)
        last = jnp.where(lane == heads + h, low.astype(jnp.float32), last)
    out_ref[:, 3 * width :] = last.astype(jnp.bfloat16)


def gathered_states(maps, heads):
    count = lax.axis_size("seq")
    place = lax.axis_index("seq")
    gathered = lax.all_gather(maps, "seq").astype(jnp.float32)

    def walk(steps, pick, rows):
        def one(lap, state):
            pair = lax.dynamic_index_in_dim(gathered, pick(lap), 0, False)[rows]
            moved = jnp.einsum("hij,hjk->hik", state, pair[:, 0], precision=highest)
            return state - moved + pair[:, 1]

        return lax.fori_loop(0, steps, one, jnp.zeros((heads,) + maps.shape[2:], jnp.float32))

    first = walk(place, lambda lap: lap, slice(0, heads))
    second = walk(count - 1 - place, lambda lap: count - 1 - lap, slice(heads, None))
    return jnp.concatenate([first, second]).astype(maps.dtype)


def states_kernel(count, heads, map_ref, out_ref, inbox, outbox, send, recv, send_back, recv_back):
    me = lax.axis_index("seq")
    barrier = pltpu.get_barrier_semaphore()
    for r in range(1, count):
        pl.semaphore_signal(
            barrier, inc=1, device_id={"seq": lax.rem(me + r, count)}, device_id_type=MESH
        )
    pl.semaphore_wait(barrier, count - 1)
    copies = []
    for r in range(1, count):
        peer = lax.rem(me + r, count)
        copy = pltpu.make_async_remote_copy(
            src_ref=map_ref.at[peer],
            dst_ref=inbox.at[r],
            send_sem=send.at[r],
            recv_sem=recv.at[r],
            device_id={"seq": peer},
            device_id_type=MESH,
        )
        copy.start()
        copies.append(copy)
    inbox[0] = map_ref[me]
    for copy in copies:
        copy.wait()
    backward = me // heads
    state = jnp.zeros(inbox.shape[2:], jnp.float32)

    def back(p):
        source = p + backward * (count - 1 - 2 * p)
        return source, pltpu.make_async_remote_copy(
            src_ref=outbox.at[p],
            dst_ref=out_ref.at[me],
            send_sem=send_back.at[p],
            recv_sem=recv_back.at[me],
            device_id={"seq": source},
            device_id_type=MESH,
        )

    for p in range(count):
        source, copy = back(p)
        outbox[p] = state.astype(outbox.dtype)

        @pl.when(source != me)
        def _():
            copy.start()

        @pl.when(source == me)
        def _():
            out_ref[me] = outbox[p]

        if p + 1 < count:
            slot = lax.rem(me - source + count, count)
            state = state - mm(split(state), (inbox[slot, 0], None)) + inbox[slot, 1].astype(
                jnp.float32
            )
    for p in range(count):
        source, copy = back(p)

        @pl.when(source != me)
        def _():
            copy.wait_send()

    for r in range(1, count):
        unit = lax.rem(me + r, count)
        pltpu.make_async_remote_copy(
            src_ref=outbox.at[r],
            dst_ref=out_ref.at[unit],
            send_sem=send_back.at[r],
            recv_sem=recv_back.at[unit],
            device_id={"seq": unit},
            device_id_type=MESH,
        ).wait_recv()


def boundary_states(maps, heads):
    count = lax.axis_size("seq")
    units, _, dim, _ = maps.shape
    if units != count:
        return gathered_states(maps, heads)
    vmem = pl.BlockSpec(memory_space=pltpu.VMEM)
    return pl.pallas_call(
        functools.partial(states_kernel, count, heads),
        out_shape=jax.ShapeDtypeStruct((units, dim, dim), maps.dtype),
        in_specs=[vmem],
        out_specs=vmem,
        scratch_shapes=[
            pltpu.VMEM(maps.shape, maps.dtype),
            pltpu.VMEM((count, dim, dim), maps.dtype),
            pltpu.SemaphoreType.DMA((count,)),
            pltpu.SemaphoreType.DMA((count,)),
            pltpu.SemaphoreType.DMA((count,)),
            pltpu.SemaphoreType.DMA((count,)),
        ],
        compiler_params=pltpu.CompilerParams(collective_id=0, has_side_effects=True),
        name="states",
    )(maps)


def per_device(tokens, w_query, w_key, w_value, w_beta, b_beta, d_out):
    token_count = tokens.shape[0]
    heads = w_beta.shape[1]
    width = w_query.shape[1]
    dim = width // heads
    f32 = jnp.float32
    q = jnp.dot(tokens, w_query, preferred_element_type=f32)
    k = jnp.dot(tokens, w_key, preferred_element_type=f32)
    v = jnp.dot(tokens, w_value, preferred_element_type=f32)
    w_last = jnp.pad(w_beta, ((0, 0), (0, LANES - heads)))
    z = jnp.dot(tokens, w_last, preferred_element_type=f32) + jnp.pad(b_beta, (0, LANES - heads))
    limit = 60 * 1024 * 1024
    params = pltpu.CompilerParams(vmem_limit_bytes=limit)
    shards, groups = lax.axis_size("seq"), lax.axis_size("head")
    columns_part = tokens.shape[1] // shards
    vmem = pl.BlockSpec(memory_space=pltpu.VMEM)
    routed = shards == 8 and columns_part % LANES == 0
    summary_shapes = (
        jax.ShapeDtypeStruct((2 * heads, 2, dim, dim), jnp.bfloat16),
        jax.ShapeDtypeStruct((heads, token_count, 4 * dim), f32),
    )
    if routed:
        maps, mid, columns = pl.pallas_call(
            functools.partial(exchange_summary_kernel, shards, heads, dim),
            out_shape=summary_shapes
            + (jax.ShapeDtypeStruct((token_count * shards, columns_part), tokens.dtype),),
            in_specs=[vmem] * 6,
            out_specs=(vmem,) * 3,
            scratch_shapes=[
                pltpu.SemaphoreType.DMA((shards - 1,)),
                pltpu.SemaphoreType.DMA((shards - 1,)),
                pltpu.SemaphoreType.DMA,
            ],
            compiler_params=pltpu.CompilerParams(
                vmem_limit_bytes=limit, collective_id=1, has_side_effects=True
            ),
            name="summary",
        )(tokens, q, k, v, z, d_out)
    else:
        columns = lax.all_to_all(tokens, "seq", split_axis=1, concat_axis=0, tiled=True)
        maps, mid = pl.pallas_call(
            functools.partial(summary_kernel, heads, dim),
            out_shape=summary_shapes,
            compiler_params=params,
            name="summary",
        )(q, k, v, z, d_out)
    states = boundary_states(maps, heads)
    grads = pl.pallas_call(
        functools.partial(gradient_kernel, heads, dim),
        out_shape=jax.ShapeDtypeStruct((token_count, 3 * width + LANES), jnp.bfloat16),
        compiler_params=params,
        name="gradient",
    )(q, k, z, d_out, mid, states)
    weights = (w_query, w_key, w_value)
    if routed:
        square = jax.ShapeDtypeStruct((columns_part, width), f32)
        d_x, grad_q, grad_k, grad_v, tail, sums = pl.pallas_call(
            functools.partial(finish_kernel, groups),
            out_shape=(
                jax.ShapeDtypeStruct((token_count, tokens.shape[1] // groups), tokens.dtype),
                square,
                square,
                square,
                jax.ShapeDtypeStruct((columns_part, LANES), f32),
                jax.ShapeDtypeStruct((1, LANES), f32),
            ),
            in_specs=[vmem] * 6,
            out_specs=(vmem,) * 6,
            scratch_shapes=[
                pltpu.VMEM((8,) + grads.shape, grads.dtype),
                pltpu.VMEM((groups, token_count, width), grads.dtype),
                pltpu.VMEM((groups, token_count, width), grads.dtype),
                pltpu.SemaphoreType.DMA((13,)),
                pltpu.SemaphoreType.DMA((13,)),
                pltpu.SemaphoreType.DMA((groups,)),
                pltpu.SemaphoreType.DMA((groups,)),
            ],
            compiler_params=pltpu.CompilerParams(
                vmem_limit_bytes=limit, collective_id=2, has_side_effects=True
            ),
            name="finish",
        )(grads, columns, *weights, w_last)
        bias = sums[0, :heads] + sums[0, heads : 2 * heads]
        return (d_x, grad_q, grad_k, grad_v, tail[:, :heads], bias)
    whole = lax.all_gather(grads, "seq", axis=0, tiled=True)
    partial = jnp.dot(grads[:, 3 * width : 3 * width + heads], w_beta.T, preferred_element_type=f32)
    for i, w in enumerate(weights):
        partial = partial + jnp.dot(
            grads[:, i * width : (i + 1) * width], w.T, preferred_element_type=f32
        )
    d_x = lax.psum_scatter(
        partial.astype(jnp.bfloat16), "head", scatter_dimension=1, tiled=True
    )

    def weight_grad(block):
        return lax.dot_general(
            columns, block, (((0,), (0,)), ((), ())), preferred_element_type=f32
        )

    found = [weight_grad(whole[:, i * width : (i + 1) * width]) for i in range(3)]
    tail = whole[:, 3 * width :]
    grad_wbeta = weight_grad(tail)[:, :heads]
    sums = jnp.sum(tail.astype(f32), 0)
    return (d_x, *found, grad_wbeta, sums[:heads] + sums[heads : 2 * heads])


def solution(mesh):
    in_specs = (
        P("seq", None),
        P(None, "head"),
        P(None, "head"),
        P(None, "head"),
        P(None, "head"),
        P("head"),
        P("seq", "head"),
    )
    out_specs = (
        P("seq", "head"),
        P("seq", "head"),
        P("seq", "head"),
        P("seq", "head"),
        P("seq", "head"),
        P("head"),
    )
    return jax.shard_map(
        per_device, mesh=mesh, in_specs=in_specs, out_specs=out_specs, check_vma=False
    )
```

```python
import functools

import jax
import jax.numpy as jnp
from jax import lax
from jax.experimental import pallas as pl
from jax.experimental.pallas import tpu as pltpu
from jax.sharding import PartitionSpec as P

epsilon = 1e-06
LANES = 128
MESH = pl.DeviceIdType.MESH
highest = lax.Precision.HIGHEST


def split(a):
    high = a.astype(jnp.bfloat16)
    return high, (a - high.astype(jnp.float32)).astype(jnp.bfloat16)


def only(a):
    return a.astype(jnp.bfloat16), None


def mm(a, b, dims=(1, 0)):
    numbers = (((dims[0],), (dims[1],)), ((), ()))
    dot = functools.partial(
        lax.dot_general, dimension_numbers=numbers, preferred_element_type=jnp.float32
    )
    total = dot(a[0], b[0])
    if b[1] is not None:
        total = total + dot(a[0], b[1])
    if a[1] is not None:
        total = total + dot(a[1], b[0])
    return total


def iotas(rows, cols):
    return (
        lax.broadcasted_iota(jnp.int32, (rows, cols), 0),
        lax.broadcasted_iota(jnp.int32, (rows, cols), 1),
    )


def invert_unit_lower(systems):
    size = systems[0].shape[0]
    base = min(size, LANES)
    row, col = iotas(base, base)
    eye = jnp.where(row == col, 1.0, 0.0).astype(jnp.float32)

    def step_mask(s):
        return (row // (2 * s) == col // (2 * s)) & (row % (2 * s) >= s) & (col % (2 * s) < s)

    count = size // base
    diagonals = [
        n[i * base : (i + 1) * base, i * base : (i + 1) * base] for n in systems for i in range(count)
    ]
    inverses = [eye - jnp.where(step_mask(1), n, 0.0) for n in diagonals]
    s = 2
    while s < base:
        mask = step_mask(s)
        parts = [split(x) for x in inverses]
        inner = [mm(split(jnp.where(mask, n, 0.0)), x) for n, x in zip(diagonals, parts)]
        outer = [mm(x, split(y)) for x, y in zip(parts, inner)]
        inverses = [x - y for x, y in zip(inverses, outer)]
        s *= 2
    grouped = [inverses[i * count : (i + 1) * count] for i in range(len(systems))]
    width = base
    while width < size:
        merged = []
        for n, blocks in zip(systems, grouped):
            joined = []
            for i in range(0, len(blocks), 2):
                first, second = blocks[i], blocks[i + 1]
                low = n[(i + 1) * width : (i + 2) * width, i * width : (i + 1) * width]
                corner = mm(split(second), split(mm(split(low), split(first))))
                joined.append(
                    jnp.concatenate(
                        [
                            jnp.concatenate([first, jnp.zeros_like(first)], 1),
                            jnp.concatenate([-corner, second], 1),
                        ],
                        0,
                    )
                )
            merged.append(joined)
        grouped = merged
        width *= 2
    return [g[0] for g in grouped]


def normalise(raw):
    scale = lax.rsqrt(jnp.sum(raw * raw, -1, keepdims=True) + epsilon)
    return raw * scale, scale


def meet(peers):
    barrier = pltpu.get_barrier_semaphore()
    for peer in peers:
        pl.semaphore_signal(barrier, inc=1, device_id=peer, device_id_type=MESH)
    pl.semaphore_wait(barrier, len(peers))


def exchange_summary_kernel(
    shards, heads, dim, x_ref, q_ref, k_ref, v_ref, z_ref, g_ref, map_ref, mid_ref, cols_ref, send, recv, here
):
    me = lax.axis_index("seq")
    rows = x_ref.shape[0]
    part = cols_ref.shape[1]
    peers = [lax.rem(me + r, shards) for r in range(1, shards)]
    meet([{"seq": p} for p in peers])

    def ends(p):
        return (
            x_ref.at[:, pl.ds(pl.multiple_of(p * part, part), part)],
            cols_ref.at[pl.ds(pl.multiple_of(me * rows, rows), rows), :],
        )

    copies = []
    for i, p in enumerate(peers):
        source, target = ends(p)
        copy = pltpu.make_async_remote_copy(
            src_ref=source,
            dst_ref=target,
            send_sem=send.at[i],
            recv_sem=recv.at[i],
            device_id={"seq": p},
            device_id_type=MESH,
        )
        copy.start()
        copies.append(copy)
    own = pltpu.make_async_copy(*ends(me), here)
    own.start()
    summary_kernel(heads, dim, q_ref, k_ref, v_ref, z_ref, g_ref, map_ref, mid_ref)
    own.wait()
    for copy in copies:
        copy.wait()


def finish_kernel(
    groups, grads_ref, cols_ref, wq_ref, wk_ref, wv_ref, wb_ref,
    dx_ref, gq_ref, gk_ref, gv_ref, tail_ref, sum_ref,
    held, piece, landed, send, recv, piece_send, piece_recv,
):
    me = lax.axis_index("seq")
    group = lax.axis_index("head")
    rows = grads_ref.shape[0]
    half = rows // 2
    width = gq_ref.shape[1]
    top, bottom = pl.ds(0, half), pl.ds(half, half)

    def other(o):
        index = me
        for bit in (1, 2, 4):
            if o & bit:
                index = index + bit - 2 * bit * ((me // bit) % 2)
        return index

    across, inner, outer = ({"seq": other(o)} for o in (1, 2, 4))
    others = [{"head": lax.rem(group + r, groups)} for r in range(1, groups)]
    meet([across, inner, outer] + others)

    def move(i, source, slot, part, device):
        return pltpu.make_async_remote_copy(
            src_ref=source.at[part, :],
            dst_ref=held.at[slot].at[part, :],
            send_sem=send.at[i],
            recv_sem=recv.at[i],
            device_id=device,
            device_id_type=MESH,
        )

    hops = [
        move(0, grads_ref, 1, pl.ds(0, rows), across),
        move(1, grads_ref, 2, top, inner),
        move(2, grads_ref, 2, bottom, inner),
        move(3, grads_ref, 4, bottom, outer),
        move(4, grads_ref, 4, top, outer),
        move(5, held.at[2], 6, top, outer),
        move(6, held.at[4], 6, bottom, inner),
        move(7, held.at[2], 3, top, across),
        move(8, held.at[2], 3, bottom, across),
        move(9, held.at[4], 5, top, across),
        move(10, held.at[4], 5, bottom, across),
        move(11, held.at[6], 7, top, across),
        move(12, held.at[6], 7, bottom, across),
    ]
    for i in (1, 3, 2, 4, 0):
        hops[i].start()

    def input_part(index):
        span = pl.ds(pl.multiple_of(index * width, width), width)
        total = lax.dot_general(
            grads_ref[:, 3 * width :], wb_ref[span, :], (((1,), (1,)), ((), ())),
            preferred_element_type=jnp.float32,
        )
        for i, w in enumerate((wq_ref, wk_ref, wv_ref)):
            total = total + lax.dot_general(
                grads_ref[:, i * width : (i + 1) * width], w[span, :], (((1,), (1,)), ((), ())),
                preferred_element_type=jnp.float32,
            )
        return total

    pieces = []
    for r in range(1, groups):
        piece[r] = input_part(lax.rem(group + r, groups)).astype(piece.dtype)
        copy = pltpu.make_async_remote_copy(
            src_ref=piece.at[r],
            dst_ref=landed.at[r],
            send_sem=piece_send.at[r],
            recv_sem=piece_recv.at[r],
            device_id=others[r - 1],
            device_id_type=MESH,
        )
        copy.start()
        pieces.append(copy)
    own = input_part(group)

    def add(o):
        block = grads_ref if o == 0 else held.at[o]
        span = pl.ds(pl.multiple_of(other(o) * rows, rows), rows)
        lhs = cols_ref[span, :].T
        for i, target in enumerate((gq_ref, gk_ref, gv_ref, tail_ref)):
            columns = slice(i * width, (i + 1) * width if i < 3 else None)
            value = jnp.dot(lhs, block[:, columns], preferred_element_type=jnp.float32)
            target[...] = value if o == 0 else target[...] + value
        total = jnp.sum(block[:, 3 * width :].astype(jnp.float32), 0, keepdims=True)
        sum_ref[...] = total if o == 0 else sum_ref[...] + total

    def arrive(i, *then):
        hops[i].wait_recv()
        for j in then:
            hops[j].start()

    add(0)
    arrive(0)
    add(1)
    arrive(1, 5, 7)
    arrive(3, 6, 10)
    arrive(2, 8)
    arrive(4, 9)
    add(2)
    add(4)
    arrive(7)
    arrive(8)
    add(3)
    arrive(9)
    arrive(10)
    add(5)
    for r, copy in enumerate(pieces, 1):
        copy.wait()
        own = own + landed[r].astype(jnp.float32)
    dx_ref[...] = own.astype(dx_ref.dtype)
    arrive(5, 11)
    arrive(6, 12)
    add(6)
    arrive(11)
    arrive(12)
    add(7)
    for hop in hops:
        hop.wait_send()


def place_kernel(count, *refs):
    sems = refs[-1]
    copies = [pltpu.make_async_copy(refs[i], refs[count + i], sems.at[i]) for i in range(count)]
    for copy in copies:
        copy.start()
    for copy in copies:
        copy.wait()


def place(arrays):
    count = len(arrays)
    return pl.pallas_call(
        functools.partial(place_kernel, count),
        out_shape=tuple(jax.ShapeDtypeStruct(a.shape, a.dtype) for a in arrays),
        in_specs=[pl.BlockSpec(memory_space=pltpu.VMEM)] * count,
        out_specs=(pl.BlockSpec(memory_space=pltpu.HBM),) * count,
        scratch_shapes=[pltpu.SemaphoreType.DMA((count,))],
        name="place",
    )(*arrays)


def summary_kernel(heads, dim, q_ref, k_ref, v_ref, z_ref, g_ref, map_ref, mid_ref):
    count = q_ref.shape[0]
    row, col = iotas(count, count)
    strict, inclusive = row > col, row >= col
    every = range(heads)
    cols = [slice(h * dim, (h + 1) * dim) for h in every]
    beta_all = 2.0 * jax.nn.sigmoid(z_ref[...])
    beta = [beta_all[:, h : h + 1] for h in every]
    qn = [normalise(q_ref[:, c])[0] for c in cols]
    kn = [normalise(k_ref[:, c])[0] for c in cols]
    ks = [split(x) for x in kn]
    qs = [split(x) for x in qn]
    gs = [(g_ref[:, c], None) for c in cols]
    gram = [jnp.where(strict, mm(x, x, (1, 1)), 0.0) for x in ks]
    inverse = [split(t) for t in invert_unit_lower([b * n for b, n in zip(beta, gram)])]
    gram = [split(n) for n in gram]
    scores = [split(jnp.where(inclusive, mm(a, b, (1, 1)), 0.0)) for a, b in zip(qs, ks)]
    back = [mm(p, g, (0, 0)) for p, g in zip(scores, gs)]
    forth_in = [jnp.concatenate([v_ref[:, c], k], 1) for c, k in zip(cols, kn)]
    forth = [split(mm(t, split(b * x))) for t, b, x in zip(inverse, beta, forth_in)]
    plain = [x - mm(n, f) for x, n, f in zip(forth_in, gram, forth)]
    adjoint = [
        mm(t, split(jnp.concatenate([p, k], 1)), (0, 0)) for t, p, k in zip(inverse, back, kn)
    ]
    ends = [mm(f, k, (0, 0)) for f, k in zip(forth, ks)]
    tails = [mm(split(a), split(b * k), (0, 0)) for a, b, k in zip(adjoint, beta, kn)]
    direct = [mm(g, q, (0, 0)) for g, q in zip(gs, qs)]
    for h in every:
        map_ref[h, 0] = ends[h][dim:].astype(map_ref.dtype)
        map_ref[h, 1] = ends[h][:dim].astype(map_ref.dtype)
        map_ref[heads + h, 0] = tails[h][dim:].astype(map_ref.dtype)
        map_ref[heads + h, 1] = (direct[h] - tails[h][:dim]).astype(map_ref.dtype)
        mid_ref[h, :, : 2 * dim] = plain[h]
        mid_ref[h, :, 2 * dim :] = adjoint[h]


def gradient_kernel(
    heads, dim, q_ref, k_ref, z_ref, g_ref, mid_ref, state_ref, out_ref
):
    count = q_ref.shape[0]
    row, col = iotas(count, count)
    strict, inclusive = row > col, row >= col
    beta_all = 2.0 * jax.nn.sigmoid(z_ref[...])
    width = heads * dim
    every = range(heads)
    cols = [slice(h * dim, (h + 1) * dim) for h in every]
    beta = [beta_all[:, h : h + 1] for h in every]
    qp = [normalise(q_ref[:, c]) for c in cols]
    kp = [normalise(k_ref[:, c]) for c in cols]
    ks = [split(x[0]) for x in kp]
    qs = [split(x[0]) for x in qp]
    gs = [(g_ref[:, c], None) for c in cols]
    ss = [(state_ref[h], None) for h in every]
    ds = [(state_ref[heads + h], None) for h in every]
    plain = [
        mid_ref[h, :, :dim] - mm(split(mid_ref[h, :, dim : 2 * dim]), ss[h], (1, 1)) for h in every
    ]
    dx = [
        mid_ref[h, :, 2 * dim : 3 * dim] + mm(split(mid_ref[h, :, 3 * dim :]), ds[h], (1, 1))
        for h in every
    ]
    us = [split(b * x) for b, x in zip(beta, plain)]
    dv = [b * x for b, x in zip(beta, dx)]
    dvs = [split(x) for x in dv]
    inner = [split(jnp.where(inclusive, mm(g, u, (1, 1)), 0.0)) for g, u in zip(gs, us)]
    pair = [jnp.where(strict, mm(d, u, (1, 1)), 0.0) for d, u in zip(dvs, us)]
    both = [split(e + e.T) for e in pair]
    dqn = [mm(g, s) + mm(i, k) for g, s, i, k in zip(gs, ss, inner, ks)]
    dkn = [
        mm(i, q, (0, 0)) + mm(u, d) - mm(x, s) - mm(e, k)
        for i, q, u, d, x, s, e, k in zip(inner, qs, us, ds, dvs, ss, both, ks)
    ]

    def through(grad, pair):
        unit, scale = pair
        return scale * (grad - unit * jnp.sum(unit * grad, -1, keepdims=True))

    lane = lax.broadcasted_iota(jnp.int32, (count, LANES), 1)
    last = jnp.zeros((count, LANES), jnp.float32)
    for h in every:
        out_ref[:, cols[h]] = through(dqn[h], qp[h]).astype(jnp.bfloat16)
        out_ref[:, width + h * dim : width + (h + 1) * dim] = through(dkn[h], kp[h]).astype(
            jnp.bfloat16
        )
        out_ref[:, 2 * width + h * dim : 2 * width + (h + 1) * dim] = dv[h].astype(jnp.bfloat16)
        dz = jnp.sum(dx[h] * plain[h], -1, keepdims=True) * beta[h] * (1.0 - 0.5 * beta[h])
        high, low = split(dz)
        last = jnp.where(lane == h, high.astype(jnp.float32), last)
        last = jnp.where(lane == heads + h, low.astype(jnp.float32), last)
    out_ref[:, 3 * width :] = last.astype(jnp.bfloat16)


def gathered_states(maps, heads):
    count = lax.axis_size("seq")
    place = lax.axis_index("seq")
    gathered = lax.all_gather(maps, "seq").astype(jnp.float32)

    def walk(steps, pick, rows):
        def one(lap, state):
            pair = lax.dynamic_index_in_dim(gathered, pick(lap), 0, False)[rows]
            moved = jnp.einsum("hij,hjk->hik", state, pair[:, 0], precision=highest)
            return state - moved + pair[:, 1]

        return lax.fori_loop(0, steps, one, jnp.zeros((heads,) + maps.shape[2:], jnp.float32))

    first = walk(place, lambda lap: lap, slice(0, heads))
    second = walk(count - 1 - place, lambda lap: count - 1 - lap, slice(heads, None))
    return jnp.concatenate([first, second]).astype(maps.dtype)


def states_kernel(count, heads, map_ref, out_ref, inbox, outbox, send, recv, send_back, recv_back):
    me = lax.axis_index("seq")
    barrier = pltpu.get_barrier_semaphore()
    for r in range(1, count):
        pl.semaphore_signal(
            barrier, inc=1, device_id={"seq": lax.rem(me + r, count)}, device_id_type=MESH
        )
    pl.semaphore_wait(barrier, count - 1)
    copies = []
    for r in range(1, count):
        peer = lax.rem(me + r, count)
        copy = pltpu.make_async_remote_copy(
            src_ref=map_ref.at[peer],
            dst_ref=inbox.at[r],
            send_sem=send.at[r],
            recv_sem=recv.at[r],
            device_id={"seq": peer},
            device_id_type=MESH,
        )
        copy.start()
        copies.append(copy)
    inbox[0] = map_ref[me]
    for copy in copies:
        copy.wait()
    backward = me // heads
    state = jnp.zeros(inbox.shape[2:], jnp.float32)

    def back(p):
        source = p + backward * (count - 1 - 2 * p)
        return source, pltpu.make_async_remote_copy(
            src_ref=outbox.at[p],
            dst_ref=out_ref.at[me],
            send_sem=send_back.at[p],
            recv_sem=recv_back.at[me],
            device_id={"seq": source},
            device_id_type=MESH,
        )

    for p in range(count):
        source, copy = back(p)
        outbox[p] = state.astype(outbox.dtype)

        @pl.when(source != me)
        def _():
            copy.start()

        @pl.when(source == me)
        def _():
            out_ref[me] = outbox[p]

        if p + 1 < count:
            slot = lax.rem(me - source + count, count)
            state = state - mm(split(state), (inbox[slot, 0], None)) + inbox[slot, 1].astype(
                jnp.float32
            )
    for p in range(count):
        source, copy = back(p)

        @pl.when(source != me)
        def _():
            copy.wait_send()

    for r in range(1, count):
        unit = lax.rem(me + r, count)
        pltpu.make_async_remote_copy(
            src_ref=outbox.at[r],
            dst_ref=out_ref.at[unit],
            send_sem=send_back.at[r],
            recv_sem=recv_back.at[unit],
            device_id={"seq": unit},
            device_id_type=MESH,
        ).wait_recv()


def boundary_states(maps, heads):
    count = lax.axis_size("seq")
    units, _, dim, _ = maps.shape
    if units != count:
        return gathered_states(maps, heads)
    vmem = pl.BlockSpec(memory_space=pltpu.VMEM)
    return pl.pallas_call(
        functools.partial(states_kernel, count, heads),
        out_shape=jax.ShapeDtypeStruct((units, dim, dim), maps.dtype),
        in_specs=[vmem],
        out_specs=vmem,
        scratch_shapes=[
            pltpu.VMEM(maps.shape, maps.dtype),
            pltpu.VMEM((count, dim, dim), maps.dtype),
            pltpu.SemaphoreType.DMA((count,)),
            pltpu.SemaphoreType.DMA((count,)),
            pltpu.SemaphoreType.DMA((count,)),
            pltpu.SemaphoreType.DMA((count,)),
        ],
        compiler_params=pltpu.CompilerParams(collective_id=0, has_side_effects=True),
        name="states",
    )(maps)


def per_device(tokens, w_query, w_key, w_value, w_beta, b_beta, d_out):
    token_count = tokens.shape[0]
    heads = w_beta.shape[1]
    width = w_query.shape[1]
    dim = width // heads
    f32 = jnp.float32
    q = jnp.dot(tokens, w_query, preferred_element_type=f32)
    k = jnp.dot(tokens, w_key, preferred_element_type=f32)
    v = jnp.dot(tokens, w_value, preferred_element_type=f32)
    w_last = jnp.pad(w_beta, ((0, 0), (0, LANES - heads)))
    z = jnp.dot(tokens, w_last, preferred_element_type=f32) + jnp.pad(b_beta, (0, LANES - heads))
    limit = 60 * 1024 * 1024
    params = pltpu.CompilerParams(vmem_limit_bytes=limit)
    shards, groups = lax.axis_size("seq"), lax.axis_size("head")
    columns_part = tokens.shape[1] // shards
    vmem = pl.BlockSpec(memory_space=pltpu.VMEM)
    routed = shards == 8 and columns_part % LANES == 0
    summary_shapes = (
        jax.ShapeDtypeStruct((2 * heads, 2, dim, dim), jnp.bfloat16),
        jax.ShapeDtypeStruct((heads, token_count, 4 * dim), f32),
    )
    if routed:
        maps, mid, columns = pl.pallas_call(
            functools.partial(exchange_summary_kernel, shards, heads, dim),
            out_shape=summary_shapes
            + (jax.ShapeDtypeStruct((token_count * shards, columns_part), tokens.dtype),),
            in_specs=[vmem] * 6,
            out_specs=(vmem,) * 3,
            scratch_shapes=[
                pltpu.SemaphoreType.DMA((shards - 1,)),
                pltpu.SemaphoreType.DMA((shards - 1,)),
                pltpu.SemaphoreType.DMA,
            ],
            compiler_params=pltpu.CompilerParams(
                vmem_limit_bytes=limit, collective_id=1, has_side_effects=True
            ),
            name="summary",
        )(tokens, q, k, v, z, d_out)
    else:
        columns = lax.all_to_all(tokens, "seq", split_axis=1, concat_axis=0, tiled=True)
        maps, mid = pl.pallas_call(
            functools.partial(summary_kernel, heads, dim),
            out_shape=summary_shapes,
            compiler_params=params,
            name="summary",
        )(q, k, v, z, d_out)
    states = boundary_states(maps, heads)
    grads = pl.pallas_call(
        functools.partial(gradient_kernel, heads, dim),
        out_shape=jax.ShapeDtypeStruct((token_count, 3 * width + LANES), jnp.bfloat16),
        compiler_params=params,
        name="gradient",
    )(q, k, z, d_out, mid, states)
    weights = (w_query, w_key, w_value)
    if routed:
        square = jax.ShapeDtypeStruct((columns_part, width), f32)
        d_x, grad_q, grad_k, grad_v, tail, sums = pl.pallas_call(
            functools.partial(finish_kernel, groups),
            out_shape=(
                jax.ShapeDtypeStruct((token_count, tokens.shape[1] // groups), tokens.dtype),
                square,
                square,
                square,
                jax.ShapeDtypeStruct((columns_part, LANES), f32),
                jax.ShapeDtypeStruct((1, LANES), f32),
            ),
            in_specs=[vmem] * 6,
            out_specs=(vmem,) * 6,
            scratch_shapes=[
                pltpu.VMEM((8,) + grads.shape, grads.dtype),
                pltpu.VMEM((groups, token_count, width), grads.dtype),
                pltpu.VMEM((groups, token_count, width), grads.dtype),
                pltpu.SemaphoreType.DMA((13,)),
                pltpu.SemaphoreType.DMA((13,)),
                pltpu.SemaphoreType.DMA((groups,)),
                pltpu.SemaphoreType.DMA((groups,)),
            ],
            compiler_params=pltpu.CompilerParams(
                vmem_limit_bytes=limit, collective_id=2, has_side_effects=True
            ),
            name="finish",
        )(grads, columns, *weights, w_last)
        bias = sums[0, :heads] + sums[0, heads : 2 * heads]
        d_x, grad_q, grad_k, grad_v = place((d_x, grad_q, grad_k, grad_v))
        return (d_x, grad_q, grad_k, grad_v, tail[:, :heads], bias)
    whole = lax.all_gather(grads, "seq", axis=0, tiled=True)
    partial = jnp.dot(grads[:, 3 * width : 3 * width + heads], w_beta.T, preferred_element_type=f32)
    for i, w in enumerate(weights):
        partial = partial + jnp.dot(
            grads[:, i * width : (i + 1) * width], w.T, preferred_element_type=f32
        )
    d_x = lax.psum_scatter(
        partial.astype(jnp.bfloat16), "head", scatter_dimension=1, tiled=True
    )

    def weight_grad(block):
        return lax.dot_general(
            columns, block, (((0,), (0,)), ((), ())), preferred_element_type=f32
        )

    found = [weight_grad(whole[:, i * width : (i + 1) * width]) for i in range(3)]
    tail = whole[:, 3 * width :]
    grad_wbeta = weight_grad(tail)[:, :heads]
    sums = jnp.sum(tail.astype(f32), 0)
    return (d_x, *found, grad_wbeta, sums[:heads] + sums[heads : 2 * heads])


def solution(mesh):
    in_specs = (
        P("seq", None),
        P(None, "head"),
        P(None, "head"),
        P(None, "head"),
        P(None, "head"),
        P("head"),
        P("seq", "head"),
    )
    out_specs = (
        P("seq", "head"),
        P("seq", "head"),
        P("seq", "head"),
        P("seq", "head"),
        P("seq", "head"),
        P("head"),
    )
    return jax.shard_map(
        per_device, mesh=mesh, in_specs=in_specs, out_specs=out_specs, check_vma=False
    )
```
